512 devices in a mesh: grp: 64 (over z, x_lo, core), rep: 8 (over y, x_hi).
Axes of the slice: x: 4 (x_hi: 2, x_lo: 2; x = x_hi * 2 + x_lo), y: 4, z: 16, core: 2. Of those that a mesh axis runs over, the one named last changes fastest.
Arguments:
- adjoint: bfloat16 [1024, 512], P('grp'), may hold values from -6 to 6
- active: int32 [1024, 512], P('grp'), may hold values 0 or 1
- counts: int32 [1024, 65536], P('rep', 'grp'), may hold values from 0 to 3, as said below
- src_degree: int32 [1024], P('rep'), may hold values from 8 to 256
- dst_degree: int32 [65536], P('grp'), may hold values from 8 to 256
- inputs: bfloat16 [65536, 512], P(('grp', 'rep')), may hold values from -6 to 6
- weight: bfloat16 [512, 512], replicated, may hold values from -0.25 to 0.25
Outputs:
- grad_input: bfloat16 [65536, 512], P(('grp', 'rep'))
- grad_weight: float32 [512, 512], P('rep')
The draws below stay inside these ranges and needn't reach their ends.
Inputs may be any that keep to these rules, and one draw needn't show every extreme that they name: Edge counts; within an aligned tile of 16 source rows by 1024 destination columns the share of nonzero entries ranges from none to all, differing from tile to tile.
All inputs are finite; a program needn't handle non-finite values. No bound on the sum of `active` on one device may be relied on, other than what follows from the above.
Results may differ from the reference program's by a relative error of at most 0.0057.
Values may be sent and summed in bfloat16 or wider, within the bound.
A program may use at most 64 MiB of HBM per device.

```python
import jax
import jax.numpy as jnp
from jax import lax

F = 512
VS = 16
VD = 1024
NSRC = 1024
NDST = 65536


def draw_counts(key, part):
    level_key, entry_key = jax.random.split(jax.random.fold_in(key, 11))
    src_blocks = NSRC // VS
    dst_blocks = NDST // VD
    levels = jax.random.randint(level_key, (src_blocks, 1, dst_blocks, 1), 0, 9)
    entries = jax.random.randint(entry_key, (src_blocks, VS, dst_blocks, VD), 0, 24)
    edges = jnp.where(entries % 8 < levels, entries // 8 + 1, 0)
    return edges.reshape(NSRC, NDST).astype(jnp.int32)


def touch_ends(result, stream_key, least, top_value):
    spot = [jax.random.randint(jax.random.fold_in(stream_key, axis), (), 0, length) for axis, length in enumerate(result.shape)]
    longest = result.shape.index(max(result.shape))
    beside = spot[:longest] + [(spot[longest] + 1) % result.shape[longest]] + spot[longest + 1:]
    return result.at[tuple(spot)].set(least).at[tuple(beside)].set(top_value)


def level_of(key, shape, shards, low, top_value):
    loudness, own = 1.0, jax.random.fold_in(key, 6)
    for axis_at, parts in shards:
        steps = jnp.exp(jax.random.uniform(jax.random.fold_in(own, axis_at), (parts,), jnp.float32, low / len(shards), top_value / len(shards)))
        loudness = loudness * jnp.repeat(steps, shape[axis_at] // parts).reshape([-1 if axis == axis_at else 1 for axis in range(len(shape))])
    return loudness


def scatter_about(own_key, extent, scale, most, cuts=(), kind=jnp.bfloat16):
    values = jax.random.normal(own_key, extent, jnp.float32) * scale
    if len(cuts) > 0:
        values = level_of(own_key, extent, cuts, -0.22, 0.18) * values
    return jnp.clip(values, min=-most, max=most).astype(kind)


def setup_inputs(seed: int = 0) -> dict:
    key_list = jax.random.split(jax.random.key(seed), 8)
    return {
        "adjoint": scatter_about(key_list[0], (NSRC, F), 1.0, 6.0, ((0, 64),)),
        "active": touch_ends((jax.random.randint(key_list[1], (NSRC, F), 0, 2) < 1).astype(jnp.int32), jax.random.fold_in(key_list[1], 1), 0, 1),
        "counts": draw_counts(jax.random.fold_in(key_list[7], 71), 0),
        "src_degree": touch_ends(jax.random.randint(key_list[3], (NSRC,), 8, 257), jax.random.fold_in(key_list[3], 1), 8, 256).astype(jnp.int32),
        "dst_degree": touch_ends(jax.random.randint(key_list[4], (NDST,), 8, 257), jax.random.fold_in(key_list[4], 1), 8, 256).astype(jnp.int32),
        "inputs": scatter_about(key_list[5], (NDST, F), 1.0, 6.0, ((0, 512),)),
        "weight": scatter_about(key_list[6], (F, F), F ** -0.5, 0.25),
    }


def reference(adjoint, active, counts, src_degree, dst_degree, inputs, weight):
    masked = (adjoint.astype(jnp.float32) * active.astype(jnp.float32)).astype(jnp.bfloat16)
    src_scale = lax.rsqrt(src_degree.astype(jnp.float32))
    dst_scale = lax.rsqrt(dst_degree.astype(jnp.float32))
    vertex_total = inputs.shape[0]
    dst_blocks = vertex_total // VD

    def one_block(block_index):
        start = (block_index * VD).astype(jnp.int32)
        count_tile = lax.dynamic_slice_in_dim(counts, start, VD, 1).astype(jnp.float32)
        col_scale = lax.dynamic_slice_in_dim(dst_scale, start, VD, 0)
        scaled_tile = (count_tile * src_scale[:, None] * col_scale[None, :]).astype(jnp.bfloat16)
        return lax.dot_general(scaled_tile, masked, (((0,), (0,)), ((), ())), preferred_element_type=jnp.float32)
    grad_pre = lax.map(one_block, jnp.arange(dst_blocks, dtype=jnp.int32)).reshape(vertex_total, F)
    grad_high = grad_pre.astype(jnp.bfloat16)
    grad_low = (grad_pre - grad_high.astype(jnp.float32)).astype(jnp.bfloat16)
    grad_input = lax.dot_general(grad_high, weight, (((1,), (1,)), ((), ())), preferred_element_type=jnp.float32).astype(jnp.bfloat16)
    upper = lax.dot_general(inputs, grad_high, (((0,), (0,)), ((), ())), preferred_element_type=jnp.float32)
    lower = lax.dot_general(inputs, grad_low, (((0,), (0,)), ((), ())), preferred_element_type=jnp.float32)
    grad_weight = (upper + lower) / vertex_total
    return (grad_input, grad_weight)
```

```python
import jax
import jax.numpy as jnp
from jax import lax
from jax.sharding import PartitionSpec as P


def body(adjoint, active, counts, src_degree, dst_degree, inputs, weight):
    masked = (adjoint.astype(jnp.float32) * active.astype(jnp.float32)).astype(jnp.bfloat16)
    src_scale = lax.rsqrt(src_degree.astype(jnp.float32))
    dst_scale = lax.rsqrt(dst_degree.astype(jnp.float32))
    scaled = (counts.astype(jnp.float32) * src_scale[:, None] * dst_scale[None, :]).astype(jnp.bfloat16)
    my_scaled = lax.all_to_all(scaled, "rep", split_axis=1, concat_axis=0, tiled=True)
    all_masked = lax.all_gather(masked, "grp", axis=0, tiled=True)
    grad_pre = lax.dot_general(
        my_scaled, all_masked, (((0,), (0,)), ((), ())), preferred_element_type=jnp.float32
    )
    high = grad_pre.astype(jnp.bfloat16)
    low = (grad_pre - high.astype(jnp.float32)).astype(jnp.bfloat16)
    grad_input = lax.dot_general(
        high, weight, (((1,), (1,)), ((), ())), preferred_element_type=jnp.float32
    ).astype(jnp.bfloat16)
    vertex_total = inputs.shape[0] * lax.axis_size("grp") * lax.axis_size("rep")
    upper = lax.dot_general(inputs, high, (((0,), (0,)), ((), ())), preferred_element_type=jnp.float32)
    lower = lax.dot_general(inputs, low, (((0,), (0,)), ((), ())), preferred_element_type=jnp.float32)
    part = lax.psum_scatter(upper + lower, "rep", scatter_dimension=0, tiled=True)
    grad_weight = lax.psum(part, "grp")
    return (grad_input, grad_weight / vertex_total)


def solution(mesh):
    in_specs = (
        P("grp", None),
        P("grp", None),
        P("rep", "grp"),
        P("rep"),
        P("grp"),
        P(("grp", "rep"), None),
        P(),
    )
    out_specs = (P(("grp", "rep"), None), P("rep", None))
    return jax.shard_map(body, mesh=mesh, in_specs=in_specs, out_specs=out_specs, check_vma=False)
```

```python
import jax
import jax.numpy as jnp
from jax import lax
from jax.experimental import pallas as pl
from jax.experimental.pallas import tpu as pltpu
from jax.sharding import PartitionSpec as P

MESH = pl.DeviceIdType.MESH
F32, BF16 = jnp.float32, jnp.bfloat16


def kernel(
    adjoint, active, counts, src_degree, dst_degree, inputs, weight,
    grad_input, grad_weight,
    masked, packed, tiles, inputs_t, half_out, half_in, own_half, plane_out, plane_in,
    ring_out, ring_in, total,
    tile_s, tile_r, mz_s, mz_r, my_s, my_r, mx_s, mx_r, mc_s, mc_r,
    half_s, half_r, plane_s, plane_r, ring_s, ring_r, tot_s, tot_r, last_s, last_r,
):
    grp, rep = lax.axis_index("grp"), lax.axis_index("rep")
    depth = masked.shape[0]
    z, quarter = lax.div(grp, 4), lax.rem(grp, 4)
    x_lo, core = lax.div(quarter, 2), lax.rem(quarter, 2)
    y, x_hi = lax.div(rep, 2), lax.rem(rep, 2)
    x = 2 * x_hi + x_lo

    def at_z(step):
        other = lax.rem(z + step, depth)
        return other, (other * 4 + quarter, rep)

    def at_plane(step):
        other_x, other_y = lax.rem(x + lax.div(step, 4), 4), lax.rem(y + lax.rem(step, 4), 4)
        other_lo = lax.rem(other_x, 2)
        other_rep = 2 * other_y + lax.div(other_x, 2)
        return other_lo, other_rep, (z * 4 + other_lo * 2 + core, other_rep)

    def at_rep(step):
        other = lax.rem(rep + step, 8)
        return other, (grp, other)

    def at_quarter(step):
        return (z * 4 + lax.rem(quarter + step, 4), rep)

    pair = (z * 4 + 2 * x_lo + 1 - core, rep)

    def copy(src, dst, send, recv, device):
        return pltpu.make_async_remote_copy(
            src_ref=src, dst_ref=dst, send_sem=send, recv_sem=recv,
            device_id=device, device_id_type=MESH,
        )

    def each(count, act):
        def turn(step, carry):
            act(step)
            return carry
        lax.fori_loop(1, count, turn, 0)

    barrier = pltpu.get_barrier_semaphore()

    def greet(device):
        pl.semaphore_signal(barrier, inc=1, device_id=device, device_id_type=MESH)

    each(16, lambda step: greet(at_plane(step)[2]))
    each(depth, lambda step: greet(at_z(step)[1]))
    greet(pair)
    greet((z * 4 + 2 * (1 - x_lo) + 1 - core, rep))

    columns = pl.ds(pl.multiple_of(y * 128, 128), 128)
    own = adjoint[:, columns].astype(F32) * active[:, columns].astype(F32)
    masked[z, quarter, :, columns] = own.astype(BF16)
    src_scale = lax.rsqrt(src_degree[...].astype(F32))
    src_scale = jnp.transpose(jnp.broadcast_to(src_scale, (128, 128)))
    dst_scale = lax.rsqrt(dst_degree[...].astype(F32))
    for part in range(8):
        cols = slice(128 * part, 128 * part + 128)
        scaled = counts[:, cols].astype(F32) * src_scale * dst_scale[:, cols]
        packed[part] = scaled.astype(BF16)
    tiles[rep] = packed[rep]
    inputs_t[...] = jnp.transpose(inputs[...])

    pl.semaphore_wait(barrier, 15 + depth - 1 + 2)

    def tile_copy(step):
        other, device = at_rep(step)
        return copy(packed.at[other], tiles.at[rep], tile_s.at[step], tile_r.at[step], device)

    def tile_wait(step):
        sender = lax.rem(rep + 8 - step, 8)
        copy(packed.at[0], tiles.at[sender], tile_s.at[step], tile_r.at[step], at_rep(step)[1]).wait_recv()

    def mz_copy(step):
        piece = masked.at[z, quarter, :, columns]
        return copy(piece, piece, mz_s.at[step], mz_r.at[step], at_z(step)[1])

    def mz_wait(step):
        sender = lax.rem(z + depth - step, depth)
        piece = masked.at[sender, quarter, :, columns]
        copy(piece, piece, mz_s.at[step], mz_r.at[step], at_z(step)[1]).wait_recv()

    def my_copy(step):
        piece = masked.at[:, quarter, :, columns]
        return copy(piece, piece, my_s.at[step], my_r.at[step], at_plane(step)[2])

    def my_wait(step):
        sender = lax.rem(y + 4 - step, 4)
        piece = masked.at[:, quarter, :, pl.ds(pl.multiple_of(sender * 128, 128), 128)]
        copy(piece, piece, my_s.at[step], my_r.at[step], at_plane(step)[2]).wait_recv()

    other_quarter = 2 * (1 - x_lo) + core
    half = depth // 2

    def mx_copy(which, at):
        piece = masked.at[pl.ds(which * half, half), at]
        return copy(piece, piece, mx_s.at[which], mx_r.at[which], at_plane(4 if which == 0 else 12)[2])

    def mc_copy(which, at):
        piece = masked.at[:, at]
        return copy(piece, piece, mc_s.at[which], mc_r.at[which], pair)

    def half_copy(lo):
        return copy(half_out.at[lo], half_in.at[lo], half_s.at[lo], half_r.at[lo], pair)

    def plane_copy(step):
        other_lo, other_rep, device = at_plane(step)
        rows = pl.ds(pl.multiple_of(other_rep * 64, 64), 64)
        return copy(plane_out.at[other_lo, rows], plane_in.at[step], plane_s.at[step], plane_r.at[step], device)

    def ring_copy(step):
        other, device = at_z(step)
        return copy(ring_out.at[other], ring_in.at[step], ring_s.at[step], ring_r.at[step], device)

    def tot_copy(step):
        piece = total.at[quarter, z]
        return copy(piece, piece, tot_s.at[step], tot_r.at[step], at_z(step)[1])

    def tot_wait(step):
        piece = total.at[quarter, lax.rem(z + depth - step, depth)]
        copy(piece, piece, tot_s.at[step], tot_r.at[step], at_z(step)[1]).wait_recv()

    def last_copy(step):
        piece = total.at[quarter]
        return copy(piece, piece, last_s.at[step], last_r.at[step], at_quarter(step))

    def last_wait(step):
        piece = total.at[lax.rem(quarter + 4 - step, 4)]
        copy(piece, piece, last_s.at[step], last_r.at[step], at_quarter(step)).wait_recv()

    each(8, lambda step: tile_copy(step).start())
    each(depth, lambda step: mz_copy(step).start())
    each(8, tile_wait)

    def term(span):
        rows = tiles[pl.ds(2 * span, 2)].reshape(256, 128)
        return lax.dot_general(
            inputs_t[...], rows, (((1,), (1,)), ((), ())), preferred_element_type=F32
        )

    for lo in range(2):
        half_out[lo] = term(2 * lo + 1 - core).astype(BF16)
        half_copy(lo).start()
    for lo in range(2):
        own_half[lo] = term(2 * lo + core)
    for lo in range(2):
        half_copy(lo).wait_recv()
        plane_out[lo] = (own_half[lo] + half_in[lo].astype(F32)).astype(BF16)
    each(16, lambda step: plane_copy(step).start())

    each(depth, mz_wait)
    each(4, lambda step: my_copy(step).start())

    rows = pl.ds(pl.multiple_of(rep * 64, 64), 64)
    summed = own_half[x_lo, rows] + half_in[x_lo, rows].astype(F32)
    each(16, lambda step: plane_copy(step).wait_recv())
    for step in range(1, 16):
        summed += plane_in[step].astype(F32)
    for side in range(2):
        ring_out[pl.ds(8 * side, 8)] = summed[:, 128 * side:128 * side + 128].reshape(8, 8, 128)
    each(depth, lambda step: ring_copy(step).start())

    each(4, my_wait)
    mx_copy(0, quarter).start()
    mx_copy(1, quarter).start()
    mc_copy(0, quarter).start()

    piece = ring_out[z]
    each(depth, lambda step: ring_copy(step).wait_recv())
    for step in range(1, depth):
        piece += ring_in[step]
    total[quarter, z] = piece
    each(depth, lambda step: tot_copy(step).start())

    mx_copy(0, other_quarter).wait_recv()
    mx_copy(1, other_quarter).wait_recv()
    mc_copy(1, other_quarter).start()
    mc_copy(0, 2 * x_lo + 1 - core).wait_recv()
    mc_copy(1, 2 * (1 - x_lo) + 1 - core).wait_recv()

    grad = jnp.zeros((128, 512), F32)
    for part in range(8):
        grad += lax.dot_general(
            jnp.transpose(tiles[part]), masked[2 * part:2 * part + 2].reshape(128, 512),
            (((1,), (0,)), ((), ())), preferred_element_type=F32,
        )
    grad_input[...] = lax.dot_general(
        grad.astype(BF16), weight[...], (((1,), (1,)), ((), ())), preferred_element_type=F32
    ).astype(BF16)

    each(depth, tot_wait)
    each(4, lambda step: last_copy(step).start())
    each(4, last_wait)
    out = jnp.zeros((64, 512), F32)
    for part in range(8):
        block = total[part // 2, 8 * (part % 2):8 * (part % 2) + 8].reshape(64, 128)
        high = block.astype(BF16)
        low = (block - high.astype(F32)).astype(BF16)
        both = lax.dot_general(
            jnp.concatenate([high, low], axis=0), masked[2 * part:2 * part + 2].reshape(128, 512),
            (((1,), (0,)), ((), ())), preferred_element_type=F32,
        )
        out += both[:64] + both[64:]
    grad_weight[...] = out * (1.0 / 65536.0)

    each(8, lambda step: tile_copy(step).wait_send())
    each(depth, lambda step: mz_copy(step).wait_send())
    each(4, lambda step: my_copy(step).wait_send())
    for which in range(2):
        mx_copy(which, quarter).wait_send()
        mc_copy(which, quarter).wait_send()
        half_copy(which).wait_send()
    each(16, lambda step: plane_copy(step).wait_send())
    each(depth, lambda step: ring_copy(step).wait_send())
    each(depth, lambda step: tot_copy(step).wait_send())
    each(4, lambda step: last_copy(step).wait_send())


def body(adjoint, active, counts, src_degree, dst_degree, inputs, weight):
    dma = pltpu.SemaphoreType.DMA
    vmem = pl.BlockSpec(memory_space=pltpu.VMEM)
    sems = []
    for count in (8, 16, 4, 2, 2, 2, 16, 16, 16, 4):
        sems += [dma((count,)), dma((count,))]
    return pl.pallas_call(
        kernel,
        out_shape=(
            jax.ShapeDtypeStruct((128, 512), BF16),
            jax.ShapeDtypeStruct((64, 512), F32),
        ),
        in_specs=[vmem] * 7,
        out_specs=(vmem, vmem),
        scratch_shapes=[
            pltpu.VMEM((16, 4, 16, 512), BF16),
            pltpu.VMEM((8, 128, 128), BF16),
            pltpu.VMEM((8, 128, 128), BF16),
            pltpu.VMEM((512, 128), BF16),
            pltpu.VMEM((2, 512, 256), BF16),
            pltpu.VMEM((2, 512, 256), BF16),
            pltpu.VMEM((2, 512, 256), F32),
            pltpu.VMEM((2, 512, 256), BF16),
            pltpu.VMEM((16, 64, 256), BF16),
            pltpu.VMEM((16, 8, 128), F32),
            pltpu.VMEM((16, 8, 128), F32),
            pltpu.VMEM((4, 16, 8, 128), F32),
        ] + sems,
        compiler_params=pltpu.CompilerParams(collective_id=0, has_side_effects=True),
    )(
        adjoint, active, counts, src_degree.reshape(1, 128), dst_degree.reshape(1, 1024),
        inputs, weight,
    )


def solution(mesh):
    in_specs = (
        P("grp", None),
        P("grp", None),
        P("rep", "grp"),
        P("rep"),
        P("grp"),
        P(("grp", "rep"), None),
        P(),
    )
    out_specs = (P(("grp", "rep"), None), P("rep", None))
    return jax.shard_map(body, mesh=mesh, in_specs=in_specs, out_specs=out_specs, check_vma=False)
```

```python
import jax
import jax.numpy as jnp
from jax import lax
from jax.experimental import pallas as pl
from jax.experimental.pallas import tpu as pltpu
from jax.sharding import PartitionSpec as P

MESH = pl.DeviceIdType.MESH
F32, BF16 = jnp.float32, jnp.bfloat16


def kernel(
    adjoint_h, active_h, counts_h, src_degree_h, dst_degree_h, inputs_h,
    high_h, sums_h,
    adjoint, active, counts, src_degree, dst_degree, inputs, high, sums,
    masked, packed, tiles, inputs_t, half_out, half_in, own_half, plane_out, plane_in,
    acc, ring_out, ring_in, total,
    load_s, save_s, token,
    tile_s, tile_r, mz_s, mz_r, my_s, my_r, mx_s, mx_r, mc_s, mc_r,
    half_s, half_r, plane_s, plane_r, ring_s, ring_r, tot_s, tot_r, cross_s, cross_r, last_s, last_r,
):
    grp, rep = lax.axis_index("grp"), lax.axis_index("rep")
    depth = masked.shape[0]
    z, quarter = lax.div(grp, 4), lax.rem(grp, 4)
    x_lo, core = lax.div(quarter, 2), lax.rem(quarter, 2)
    y, x_hi = lax.div(rep, 2), lax.rem(rep, 2)
    x = 2 * x_hi + x_lo
    across = 2 * (1 - x_lo) + core

    def at_z(step):
        other = lax.rem(z + step, depth)
        return other, (other * 4 + quarter, rep)

    def at_cross(step):
        return (lax.rem(z + step, depth) * 4 + across, rep)

    def at_plane(step):
        other_x, other_y = lax.rem(x + lax.div(step, 4), 4), lax.rem(y + lax.rem(step, 4), 4)
        other_lo = lax.rem(other_x, 2)
        other_rep = 2 * other_y + lax.div(other_x, 2)
        return other_lo, other_rep, (z * 4 + other_lo * 2 + core, other_rep)

    def at_rep(step):
        other = lax.rem(rep + step, 8)
        return other, (grp, other)

    pair = (z * 4 + 2 * x_lo + 1 - core, rep)

    def copy(src, dst, send, recv, device):
        return pltpu.make_async_remote_copy(
            src_ref=src, dst_ref=dst, send_sem=send, recv_sem=recv,
            device_id=device, device_id_type=MESH,
        )

    def each(low, count, act):
        def turn(step, carry):
            act(step)
            return carry
        lax.fori_loop(low, count, turn, 0)

    loads = [
        pltpu.make_async_copy(src, dst, load_s.at[index])
        for index, (src, dst) in enumerate((
            (counts_h, counts), (src_degree_h, src_degree), (dst_degree_h, dst_degree),
            (inputs_h, inputs), (adjoint_h, adjoint), (active_h, active),
        ))
    ]
    for load in loads:
        load.start()

    barrier = pltpu.get_barrier_semaphore()

    def greet(device):
        pl.semaphore_signal(barrier, inc=1, device_id=device, device_id_type=MESH)

    each(1, 16, lambda step: greet(at_plane(step)[2]))
    greet(pair)
    each(1, 5, lambda step: greet(at_z(step)[1]))
    each(depth - 4, depth, lambda step: greet(at_z(step)[1]))

    for load in loads[:3]:
        load.wait()
    src_scale = lax.rsqrt(src_degree[...].astype(F32))
    src_scale = jnp.transpose(jnp.broadcast_to(src_scale, (128, 128)))
    dst_scale = lax.rsqrt(dst_degree[...].astype(F32))
    for part in range(8):
        cols = slice(128 * part, 128 * part + 128)
        scaled = counts[:, cols].astype(F32) * src_scale * dst_scale[:, cols]
        packed[part] = scaled.astype(BF16)
    tiles[rep] = packed[rep]
    for load in loads[3:]:
        load.wait()
    turned = jnp.transpose(inputs[...])
    for part in range(8):
        for spot in range(4):
            at = 128 * (spot // 2) + 16 * part
            inputs_t[spot % 2, at:at + 16] = turned[64 * part + 16 * spot:64 * part + 16 * spot + 16]
    columns = pl.ds(pl.multiple_of(y * 128, 128), 128)
    own = adjoint[:, columns].astype(F32) * active[:, columns].astype(F32)
    masked[z, quarter, :, columns] = own.astype(BF16)

    pl.semaphore_wait(barrier, 15 + 1 + 8)

    def tile_copy(step):
        other, device = at_rep(step)
        return copy(packed.at[other], tiles.at[rep], tile_s.at[step], tile_r.at[step], device)

    def tile_wait(step):
        sender = lax.rem(rep + 8 - step, 8)
        copy(packed.at[0], tiles.at[sender], tile_s.at[step], tile_r.at[step], at_rep(step)[1]).wait_recv()

    def mz_copy(step):
        piece = masked.at[z, quarter, :, columns]
        return copy(piece, piece, mz_s.at[step], mz_r.at[step], at_z(step)[1])

    def mz_wait(step):
        piece = masked.at[lax.rem(z + depth - step, depth), quarter, :, columns]
        copy(piece, piece, mz_s.at[step], mz_r.at[step], at_z(step)[1]).wait_recv()

    def columns_of(which):
        return pl.ds(pl.multiple_of(which * 128, 128), 128)

    def my_copy(step):
        piece = masked.at[:, quarter, :, columns]
        return copy(piece, piece, my_s.at[step], my_r.at[step], at_plane(step)[2])

    def my_wait(step):
        piece = masked.at[:, quarter, :, columns_of(lax.rem(y + 4 - step, 4))]
        copy(piece, piece, my_s.at[step], my_r.at[step], at_plane(step)[2]).wait_recv()

    half = depth // 2

    def mx_copy(step):
        which, turn = lax.div(step, 4), lax.rem(step, 4)
        piece = masked.at[pl.ds(which * half, half), quarter, :, columns]
        return copy(piece, piece, mx_s.at[step], mx_r.at[step], at_plane(4 + 8 * which + turn)[2])

    def mx_wait(step):
        which, turn = lax.div(step, 4), lax.rem(step, 4)
        piece = masked.at[pl.ds(which * half, half), across, :, columns_of(lax.rem(y + 4 - turn, 4))]
        copy(piece, piece, mx_s.at[step], mx_r.at[step], at_plane(4 + 8 * which + turn)[2]).wait_recv()

    def mc_copy(which, at):
        piece = masked.at[:, at]
        return copy(piece, piece, mc_s.at[which], mc_r.at[which], pair)

    def half_copy(step):
        return copy(half_out.at[step], half_in.at[step], half_s.at[step], half_r.at[step], pair)

    def plane_copy(step, part, owner):
        other_lo, other_rep, device = at_plane(step)
        rows = pl.ds(pl.multiple_of((other_lo * 8 + other_rep) * 16, 16), 16)
        return copy(plane_out.at[part, rows], plane_in.at[step, owner], plane_s.at[step], plane_r.at[step], device)

    def plane_all(step):
        return copy(plane_in.at[step], plane_in.at[step], plane_s.at[step], plane_r.at[step], at_plane(step)[2])

    def ring_copy(step):
        other, device = at_z(step)
        return copy(ring_out.at[other], ring_in.at[step], ring_s.at[step], ring_r.at[step], device)

    def tot_copy(step):
        piece = total.at[quarter, z]
        return copy(piece, piece, tot_s.at[step], tot_r.at[step], at_z(step)[1])

    def tot_wait(step):
        piece = total.at[quarter, lax.rem(z + depth - step, depth)]
        copy(piece, piece, tot_s.at[step], tot_r.at[step], at_z(step)[1]).wait_recv()

    def cross_copy(step):
        piece = total.at[quarter, z]
        return copy(piece, piece, cross_s.at[step], cross_r.at[step], at_cross(step))

    def cross_wait(step):
        piece = total.at[across, lax.rem(z + depth - step, depth)]
        copy(piece, piece, cross_s.at[step], cross_r.at[step], at_cross(step)).wait_recv()

    def last_copy(which, at):
        piece = total.at[at]
        return copy(piece, piece, last_s.at[which], last_r.at[which], pair)

    each(1, 8, lambda step: tile_copy(step).start())
    for step in (4, depth - 4):
        pl.semaphore_signal(token, inc=1, device_id=at_z(step)[1], device_id_type=MESH)

    mine = pl.ds(pl.multiple_of((x_lo * 8 + rep) * 16, 16), 16)

    def term(side, owner):
        return lax.dot_general(
            inputs_t[side], tiles[owner], (((1,), (1,)), ((), ())), preferred_element_type=F32
        )

    def settle(step):
        owner = lax.rem(rep + 8 - step, 8)
        half_copy(step).wait_recv()
        plane_out[step] = (own_half[step] + half_in[step].astype(F32)).astype(BF16)
        each(1, 16, lambda other: plane_copy(other, step, owner).start())
        acc[pl.ds(pl.multiple_of(owner * 16, 16), 16)] = (
            own_half[step, mine] + half_in[step, mine].astype(F32)
        )

    for step in range(8):
        if step > 0:
            tile_wait(step)
        owner = lax.rem(rep + 8 - step, 8)
        half_out[step] = term(1 - core, owner).astype(BF16)
        half_copy(step).start()
        own_half[step] = term(core, owner)
        if step > 0:
            settle(step - 1)
        if step == 1:
            pl.semaphore_wait(token, 2)
            each(1, depth, lambda other: mz_copy(other).start())
    settle(7)

    each(1, depth, mz_wait)
    each(1, 4, lambda step: my_copy(step).start())
    each(0, 8, lambda step: mx_copy(step).start())

    summed = acc[...].reshape(8, 16, 128)
    each(1, 16, lambda step: plane_all(step).wait_recv())
    for step in range(1, 16):
        summed += plane_in[step].astype(F32)
    acc[...] = summed.reshape(128, 128)
    for row in range(depth):
        ring_out[row] = acc[pl.ds(row, 8, stride=16), :]
    each(1, depth, lambda step: ring_copy(step).start())

    each(1, 4, my_wait)
    mc_copy(0, quarter).start()
    each(0, 8, mx_wait)
    mc_copy(1, across).start()
    mc_copy(0, 2 * x_lo + 1 - core).wait_recv()
    mc_copy(1, 2 * (1 - x_lo) + 1 - core).wait_recv()

    piece = ring_out[z]
    each(1, depth, lambda step: ring_copy(step).wait_recv())
    for step in range(1, depth):
        piece += ring_in[step]
    upper = piece.astype(BF16)
    lower = (piece - upper.astype(F32)).astype(BF16)
    both = jnp.concatenate([upper, lower], axis=0)
    which_row = lax.rem(lax.broadcasted_iota(jnp.int32, (16, 512), 0), 8)
    product = jnp.zeros((16, 512), F32)
    for part in range(8):
        block = lax.dot_general(
            both, masked[2 * part:2 * part + 2].reshape(128, 512),
            (((1,), (0,)), ((), ())), preferred_element_type=F32,
        )
        product += jnp.where(which_row == part, block, 0.0)
    total[quarter, z] = jnp.sum(product, axis=0, keepdims=True)
    each(0, depth, lambda step: cross_copy(step).start())
    each(1, depth, lambda step: tot_copy(step).start())

    grad = jnp.zeros((128, 512), F32)
    for part in range(8):
        grad += lax.dot_general(
            jnp.transpose(tiles[part]), masked[2 * part:2 * part + 2].reshape(128, 512),
            (((1,), (0,)), ((), ())), preferred_element_type=F32,
        )
    high[...] = grad.astype(BF16)
    save_high = pltpu.make_async_copy(high, high_h, save_s.at[0])
    save_high.start()

    each(1, depth, tot_wait)
    last_copy(0, quarter).start()
    each(0, depth, cross_wait)
    last_copy(1, across).start()
    last_copy(0, 2 * x_lo + 1 - core).wait_recv()
    last_copy(1, 2 * (1 - x_lo) + 1 - core).wait_recv()
    for spot in range(4):
        for row in range(depth):
            at = 16 * spot + row
            sums[at:at + 1, :] = total[spot, row]
    save_sums = pltpu.make_async_copy(sums, sums_h, save_s.at[1])
    save_sums.start()

    each(1, 8, lambda step: tile_copy(step).wait_send())
    each(1, depth, lambda step: mz_copy(step).wait_send())
    each(1, 4, lambda step: my_copy(step).wait_send())
    each(0, 8, lambda step: mx_copy(step).wait_send())
    each(0, 8, lambda step: half_copy(step).wait_send())
    for which in range(2):
        mc_copy(which, quarter).wait_send()
        last_copy(which, quarter).wait_send()
    each(1, 16, lambda step: plane_all(step).wait_send())
    each(1, depth, lambda step: ring_copy(step).wait_send())
    each(1, depth, lambda step: tot_copy(step).wait_send())
    each(0, depth, lambda step: cross_copy(step).wait_send())
    save_high.wait()
    save_sums.wait()


def body(adjoint, active, counts, src_degree, dst_degree, inputs, weight):
    dma = pltpu.SemaphoreType.DMA
    anywhere = pl.BlockSpec(memory_space=pl.ANY)
    sems = [dma((6,)), dma((2,)), pltpu.SemaphoreType.REGULAR]
    for count in (8, 16, 4, 8, 2, 8, 16, 16, 16, 16, 2):
        sems += [dma((count,)), dma((count,))]
    I32 = jnp.int32
    high, sums = pl.pallas_call(
        kernel,
        out_shape=(
            jax.ShapeDtypeStruct((128, 512), BF16),
            jax.ShapeDtypeStruct((64, 512), F32),
        ),
        in_specs=[anywhere] * 6,
        out_specs=(anywhere, anywhere),
        scratch_shapes=[
            pltpu.VMEM(shape, kind) for shape, kind in (
                ((16, 512), BF16), ((16, 512), I32), ((128, 1024), I32), ((1, 128), I32),
                ((1, 1024), I32), ((128, 512), BF16), ((128, 512), BF16), ((64, 512), F32),
                ((16, 4, 16, 512), BF16),
                ((8, 128, 128), BF16),
                ((8, 128, 128), BF16),
                ((2, 256, 128), BF16),
                ((8, 256, 128), BF16),
                ((8, 256, 128), BF16),
                ((8, 256, 128), F32),
                ((8, 256, 128), BF16),
                ((16, 8, 16, 128), BF16),
                ((128, 128), F32),
                ((16, 8, 128), F32),
                ((16, 8, 128), F32),
                ((4, 16, 1, 512), F32),
            )
        ] + sems,
        compiler_params=pltpu.CompilerParams(collective_id=0, has_side_effects=True),
    )(
        adjoint, active, counts, src_degree.reshape(1, 128), dst_degree.reshape(1, 1024), inputs,
    )
    grad_input = lax.dot_general(
        high, weight, (((1,), (1,)), ((), ())), preferred_element_type=F32
    ).astype(BF16)
    return grad_input, sums * (1.0 / 65536.0)


def solution(mesh):
    in_specs = (
        P("grp", None),
        P("grp", None),
        P("rep", "grp"),
        P("rep"),
        P("grp"),
        P(("grp", "rep"), None),
        P(),
    )
    out_specs = (P(("grp", "rep"), None), P("rep", None))
    return jax.shard_map(body, mesh=mesh, in_specs=in_specs, out_specs=out_specs, check_vma=False)
```

```python
import jax
import jax.numpy as jnp
from jax import lax
from jax.experimental import pallas as pl
from jax.experimental.pallas import tpu as pltpu
from jax.sharding import PartitionSpec as P

MESH = pl.DeviceIdType.MESH
F32, BF16 = jnp.float32, jnp.bfloat16


def ring_far(step, size):
    return min(step, size - step)


PLANE_FAR = sorted(range(1, 16), key=lambda step: -ring_far(step // 4, 4) - ring_far(step % 4, 4))
Z_FAR = sorted(range(1, 16), key=lambda step: -ring_far(step, 16))
REP_NEAR = sorted(range(8), key=lambda step: ring_far(step // 2, 4) + 2 * (step % 2))


def kernel(
    adjoint_h, active_h, counts_h, src_degree_h, dst_degree_h, inputs_h, weight_h,
    grad_input, sums,
    adjoint, active, counts, src_degree, dst_degree, inputs, weight,
    masked, packed, tiles, inputs_t, half_out, half_in, own_half, plane_out, plane_in,
    acc, ring_out, ring_in, total,
    load_s, token,
    tile_s, tile_r, mz_s, mz_r, my_s, my_r, mx_s, mx_r, mc_s, mc_r,
    half_s, half_r, plane_s, plane_r, ring_s, ring_r, tot_s, tot_r, cross_s, cross_r, last_s, last_r,
):
    grp, rep = lax.axis_index("grp"), lax.axis_index("rep")
    depth = masked.shape[0]
    z, quarter = lax.div(grp, 4), lax.rem(grp, 4)
    x_lo, core = lax.div(quarter, 2), lax.rem(quarter, 2)
    y, x_hi = lax.div(rep, 2), lax.rem(rep, 2)
    x = 2 * x_hi + x_lo
    across = 2 * (1 - x_lo) + core

    def at_z(step):
        other = lax.rem(z + step, depth)
        return other, (other * 4 + quarter, rep)

    def at_cross(step):
        return (lax.rem(z + step, depth) * 4 + across, rep)

    def at_plane(step):
        other_x, other_y = lax.rem(x + lax.div(step, 4), 4), lax.rem(y + lax.rem(step, 4), 4)
        other_lo = lax.rem(other_x, 2)
        other_rep = 2 * other_y + lax.div(other_x, 2)
        return other_lo, other_rep, (z * 4 + other_lo * 2 + core, other_rep)

    def rep_at(step, way):
        turn, flip = step // 2, step % 2
        return 2 * lax.rem(y + (turn if way > 0 else 4 - turn), 4) + lax.rem(x_hi + flip, 2)

    def at_rep(step):
        other = rep_at(step, 1)
        return other, (grp, other)

    pair = (z * 4 + 2 * x_lo + 1 - core, rep)

    def copy(src, dst, send, recv, device):
        return pltpu.make_async_remote_copy(
            src_ref=src, dst_ref=dst, send_sem=send, recv_sem=recv,
            device_id=device, device_id_type=MESH,
        )

    def each(low, count, act):
        def turn(step, carry):
            act(step)
            return carry
        lax.fori_loop(low, count, turn, 0)

    barrier = pltpu.get_barrier_semaphore()

    def greet(device):
        pl.semaphore_signal(barrier, inc=1, device_id=device, device_id_type=MESH)

    loads = [
        pltpu.make_async_copy(src, dst, load_s.at[index])
        for index, (src, dst) in enumerate((
            (counts_h, counts), (src_degree_h, src_degree), (dst_degree_h, dst_degree),
            (inputs_h, inputs), (adjoint_h, adjoint), (active_h, active),
            (weight_h, weight),
        ))
    ]
    for load in loads[:3]:
        load.start()
    planes = {step: at_plane(step) for step in range(1, 16)}
    for step in (4, 12):
        greet(at_z(step)[1])
    for step in PLANE_FAR:
        greet(planes[step][2])
    for step in (3, 13, 2, 14, 1, 15):
        greet(at_z(step)[1])
    greet(pair)
    for load in loads[3:]:
        load.start()

    for load in loads[:3]:
        load.wait()
    src_scale = lax.rsqrt(src_degree[...].astype(F32))
    src_scale = jnp.transpose(jnp.broadcast_to(src_scale, (128, 128)))
    dst_scale = lax.rsqrt(dst_degree[...].astype(F32))
    for part in range(8):
        cols = slice(128 * part, 128 * part + 128)
        scaled = counts[:, cols].astype(F32) * src_scale * dst_scale[:, cols]
        packed[part] = scaled.astype(BF16)
    tiles[rep] = packed[rep]
    pl.semaphore_wait(barrier, 15 + 1 + 8)

    def tile_copy(step):
        other, device = at_rep(step)
        return copy(packed.at[other], tiles.at[rep], tile_s.at[step], tile_r.at[step], device)

    def tile_wait(step):
        sender = rep_at(step, -1)
        copy(packed.at[0], tiles.at[sender], tile_s.at[step], tile_r.at[step], at_rep(step)[1]).wait_recv()

    def mz_copy(step):
        piece = masked.at[z, quarter, :, columns]
        return copy(piece, piece, mz_s.at[step], mz_r.at[step], at_z(step)[1])

    def mz_wait(step):
        piece = masked.at[lax.rem(z + depth - step, depth), quarter, :, columns]
        copy(piece, piece, mz_s.at[step], mz_r.at[step], at_z(step)[1]).wait_recv()

    def columns_of(which):
        return pl.ds(pl.multiple_of(which * 128, 128), 128)

    def my_copy(step):
        piece = masked.at[:, quarter, :, columns]
        return copy(piece, piece, my_s.at[step], my_r.at[step], at_plane(step)[2])

    def my_wait(step):
        piece = masked.at[:, quarter, :, columns_of(lax.rem(y + 4 - step, 4))]
        copy(piece, piece, my_s.at[step], my_r.at[step], at_plane(step)[2]).wait_recv()

    half = depth // 2

    def mx_copy(step):
        which, turn = lax.div(step, 4), lax.rem(step, 4)
        piece = masked.at[pl.ds(which * half, half), quarter, :, columns]
        return copy(piece, piece, mx_s.at[step], mx_r.at[step], at_plane(4 + 8 * which + turn)[2])

    def mx_wait(step):
        which, turn = lax.div(step, 4), lax.rem(step, 4)
        piece = masked.at[pl.ds(which * half, half), across, :, columns_of(lax.rem(y + 4 - turn, 4))]
        copy(piece, piece, mx_s.at[step], mx_r.at[step], at_plane(4 + 8 * which + turn)[2]).wait_recv()

    def mc_copy(which, at):
        piece = masked.at[:, at]
        return copy(piece, piece, mc_s.at[which], mc_r.at[which], pair)

    def half_copy(step):
        return copy(half_out.at[step], half_in.at[step], half_s.at[step], half_r.at[step], pair)

    def plane_copy(step, part, owner):
        other_lo, other_rep, device = planes[step]
        rows = pl.ds(pl.multiple_of((other_lo * 8 + other_rep) * 16, 16), 16)
        return copy(plane_out.at[part, rows], plane_in.at[step, owner], plane_s.at[step], plane_r.at[step], device)

    def plane_all(step):
        return copy(plane_in.at[step], plane_in.at[step], plane_s.at[step], plane_r.at[step], at_plane(step)[2])

    def ring_copy(step):
        other, device = at_z(step)
        return copy(ring_out.at[other], ring_in.at[step], ring_s.at[step], ring_r.at[step], device)

    def tot_copy(step):
        piece = total.at[quarter, z]
        return copy(piece, piece, tot_s.at[step], tot_r.at[step], at_z(step)[1])

    def tot_wait(step):
        piece = total.at[quarter, lax.rem(z + depth - step, depth)]
        copy(piece, piece, tot_s.at[step], tot_r.at[step], at_z(step)[1]).wait_recv()

    def cross_copy(step):
        piece = total.at[quarter, z]
        return copy(piece, piece, cross_s.at[step], cross_r.at[step], at_cross(step))

    def cross_wait(step):
        piece = total.at[across, lax.rem(z + depth - step, depth)]
        copy(piece, piece, cross_s.at[step], cross_r.at[step], at_cross(step)).wait_recv()

    def last_copy(which, at):
        piece = total.at[at]
        return copy(piece, piece, last_s.at[which], last_r.at[which], pair)

    for step in reversed(REP_NEAR[1:]):
        tile_copy(step).start()
    for step in (4, depth - 4):
        pl.semaphore_signal(token, inc=1, device_id=at_z(step)[1], device_id_type=MESH)

    for load in loads[3:6]:
        load.wait()
    turned = jnp.transpose(inputs[...])
    for part in range(8):
        for spot in range(4):
            at = 128 * (spot // 2) + 16 * part
            inputs_t[spot % 2, at:at + 16] = turned[64 * part + 16 * spot:64 * part + 16 * spot + 16]
    columns = pl.ds(pl.multiple_of(y * 128, 128), 128)
    own = adjoint[:, columns].astype(F32) * active[:, columns].astype(F32)
    masked[z, quarter, :, columns] = own.astype(BF16)

    mine = pl.ds(pl.multiple_of((x_lo * 8 + rep) * 16, 16), 16)

    def term(side, owner):
        return lax.dot_general(
            inputs_t[side], tiles[owner], (((1,), (1,)), ((), ())), preferred_element_type=F32
        )

    def settle(step):
        owner = rep_at(REP_NEAR[step], -1)
        half_copy(step).wait_recv()
        plane_out[step] = (own_half[step] + half_in[step].astype(F32)).astype(BF16)
        for other in PLANE_FAR:
            plane_copy(other, step, owner).start()
        acc[pl.ds(pl.multiple_of(owner * 16, 16), 16)] = (
            own_half[step, mine] + half_in[step, mine].astype(F32)
        )

    for step in range(8):
        if step > 0:
            tile_wait(REP_NEAR[step])
        owner = rep_at(REP_NEAR[step], -1)
        half_out[step] = term(1 - core, owner).astype(BF16)
        half_copy(step).start()
        own_half[step] = term(core, owner)
        if step > 0:
            settle(step - 1)
        if step == 1:
            pl.semaphore_wait(token, 2)
            for other in Z_FAR:
                mz_copy(other).start()
    settle(7)

    each(1, depth, mz_wait)
    each(1, 4, lambda step: my_copy(step).start())
    each(0, 8, lambda step: mx_copy(step).start())

    summed = acc[...].reshape(8, 16, 128)
    for step in reversed(PLANE_FAR):
        plane_all(step).wait_recv()
        summed += plane_in[step].astype(F32)
    acc[...] = summed.reshape(128, 128)
    for row in range(depth):
        ring_out[row] = acc[pl.ds(row, 8, stride=16), :]
    for step in Z_FAR:
        ring_copy(step).start()

    each(1, 4, my_wait)
    mc_copy(0, quarter).start()
    each(0, 8, mx_wait)
    mc_copy(1, across).start()
    mc_copy(0, 2 * x_lo + 1 - core).wait_recv()
    mc_copy(1, 2 * (1 - x_lo) + 1 - core).wait_recv()

    piece = ring_out[z]
    for step in reversed(Z_FAR):
        ring_copy(step).wait_recv()
        piece += ring_in[step]
    upper = piece.astype(BF16)
    lower = (piece - upper.astype(F32)).astype(BF16)
    both = jnp.concatenate([upper, lower], axis=0)
    which_row = lax.rem(lax.broadcasted_iota(jnp.int32, (16, 512), 0), 8)
    product = jnp.zeros((16, 512), F32)
    for part in range(8):
        block = lax.dot_general(
            both, masked[2 * part:2 * part + 2].reshape(128, 512),
            (((1,), (0,)), ((), ())), preferred_element_type=F32,
        )
        product += jnp.where(which_row == part, block, 0.0)
    total[quarter, z] = jnp.sum(product, axis=0, keepdims=True) * (1.0 / 65536.0)
    for step in Z_FAR:
        cross_copy(step).start()
        tot_copy(step).start()
    cross_copy(0).start()

    grad = jnp.zeros((128, 512), F32)
    for part in range(8):
        grad += lax.dot_general(
            jnp.transpose(tiles[part]), masked[2 * part:2 * part + 2].reshape(128, 512),
            (((1,), (0,)), ((), ())), preferred_element_type=F32,
        )
    loads[6].wait()
    grad_input[...] = lax.dot_general(
        grad.astype(BF16), weight[...], (((1,), (1,)), ((), ())), preferred_element_type=F32
    ).astype(BF16)

    each(1, depth, tot_wait)
    last_copy(0, quarter).start()
    each(0, depth, cross_wait)
    last_copy(1, across).start()
    last_copy(0, 2 * x_lo + 1 - core).wait_recv()
    last_copy(1, 2 * (1 - x_lo) + 1 - core).wait_recv()
    for spot in range(4):
        for row in range(depth):
            at = 16 * spot + row
            sums[at:at + 1, :] = total[spot, row]

    each(1, 8, lambda step: tile_copy(step).wait_send())
    each(1, depth, lambda step: mz_copy(step).wait_send())
    each(1, 4, lambda step: my_copy(step).wait_send())
    each(0, 8, lambda step: mx_copy(step).wait_send())
    each(0, 8, lambda step: half_copy(step).wait_send())
    for which in range(2):
        mc_copy(which, quarter).wait_send()
        last_copy(which, quarter).wait_send()
    each(1, 16, lambda step: plane_all(step).wait_send())
    each(1, depth, lambda step: ring_copy(step).wait_send())
    each(1, depth, lambda step: tot_copy(step).wait_send())
    each(0, depth, lambda step: cross_copy(step).wait_send())


def store(near_input, near_weight, far_input, far_weight, done):
    copies = (
        pltpu.make_async_copy(near_input, far_input, done.at[0]),
        pltpu.make_async_copy(near_weight, far_weight, done.at[1]),
    )
    for copy in copies:
        copy.start()
    for copy in copies:
        copy.wait()


def body(adjoint, active, counts, src_degree, dst_degree, inputs, weight):
    dma = pltpu.SemaphoreType.DMA
    far, near = pl.BlockSpec(memory_space=pltpu.HBM), pl.BlockSpec(memory_space=pltpu.VMEM)
    sems = [dma((7,)), pltpu.SemaphoreType.REGULAR]
    for count in (8, 16, 4, 8, 2, 8, 16, 16, 16, 16, 2):
        sems += [dma((count,)), dma((count,))]
    I32 = jnp.int32
    results = (pltpu.VMEM((128, 512), BF16), pltpu.VMEM((64, 512), F32))
    grad_input, sums = pl.pallas_call(
        kernel,
        out_shape=results,
        in_specs=[far] * 7,
        out_specs=(near, near),
        scratch_shapes=[
            pltpu.VMEM(shape, kind) for shape, kind in (
                ((16, 512), BF16), ((16, 512), I32), ((128, 1024), I32), ((1, 128), I32),
                ((1, 1024), I32), ((128, 512), BF16), ((512, 512), BF16),
                ((16, 4, 16, 512), BF16),
                ((8, 128, 128), BF16),
                ((8, 128, 128), BF16),
                ((2, 256, 128), BF16),
                ((8, 256, 128), BF16),
                ((8, 256, 128), BF16),
                ((8, 256, 128), F32),
                ((8, 256, 128), BF16),
                ((16, 8, 16, 128), BF16),
                ((128, 128), F32),
                ((16, 8, 128), F32),
                ((16, 8, 128), F32),
                ((4, 16, 1, 512), F32),
            )
        ] + sems,
        compiler_params=pltpu.CompilerParams(
            collective_id=0, has_side_effects=True, vmem_limit_bytes=56 * 1024 * 1024
        ),
    )(
        adjoint, active, counts, src_degree.reshape(1, 128), dst_degree.reshape(1, 1024), inputs,
        weight,
    )
    return tuple(pl.pallas_call(
        store,
        out_shape=(
            jax.ShapeDtypeStruct((128, 512), BF16),
            jax.ShapeDtypeStruct((64, 512), F32),
        ),
        in_specs=[near, near],
        out_specs=(far, far),
        scratch_shapes=[dma((2,))], compiler_params=pltpu.CompilerParams(vmem_limit_bytes=1024 * 1024),
    )(grad_input, sums))


def solution(mesh):
    in_specs = (
        P("grp", None),
        P("grp", None),
        P("rep", "grp"),
        P("rep"),
        P("grp"),
        P(("grp", "rep"), None),
        P(),
    )
    out_specs = (P(("grp", "rep"), None), P("rep", None))
    return jax.shard_map(body, mesh=mesh, in_specs=in_specs, out_specs=out_specs, check_vma=False)
```

```python
import jax
import jax.numpy as jnp
from jax import lax
from jax.experimental import pallas as pl
from jax.experimental.pallas import tpu as pltpu
from jax.sharding import PartitionSpec as P

MESH = pl.DeviceIdType.MESH
F32, BF16 = jnp.float32, jnp.bfloat16


def ring_far(step, size):
    return min(step, size - step)


PLANE_FAR = sorted(range(1, 16), key=lambda step: -ring_far(step // 4, 4) - ring_far(step % 4, 4))
Z_FAR = sorted(range(1, 16), key=lambda step: -ring_far(step, 16))
REP_NEAR = sorted(range(8), key=lambda step: ring_far(step // 2, 4) + 2 * (step % 2))


def kernel(
    adjoint_h, active_h, counts_h, src_degree_h, dst_degree_h, inputs_h, weight_h,
    grad_input, sums,
    adjoint, active, counts, src_degree, dst_degree, inputs, weight,
    masked, packed, tiles, inputs_t, half_out, half_in, own_half, plane_out, plane_in,
    acc, ring_out, ring_in, total,
    load_s, token,
    tile_s, tile_r, mz_s, mz_r, my_s, my_r, mx_s, mx_r, mc_s, mc_r,
    half_s, half_r, plane_s, plane_r, ring_s, ring_r, tot_s, tot_r, cross_s, cross_r, last_s, last_r,
):
    grp, rep = lax.axis_index("grp"), lax.axis_index("rep")
    depth = masked.shape[0]
    z, quarter = lax.div(grp, 4), lax.rem(grp, 4)
    x_lo, core = lax.div(quarter, 2), lax.rem(quarter, 2)
    y, x_hi = lax.div(rep, 2), lax.rem(rep, 2)
    x = 2 * x_hi + x_lo
    across = 2 * (1 - x_lo) + core

    def at_z(step):
        other = lax.rem(z + step, depth)
        return other, (other * 4 + quarter, rep)

    def at_cross(step):
        return (lax.rem(z + step, depth) * 4 + across, rep)

    def at_plane(step):
        other_x, other_y = lax.rem(x + lax.div(step, 4), 4), lax.rem(y + lax.rem(step, 4), 4)
        other_lo = lax.rem(other_x, 2)
        other_rep = 2 * other_y + lax.div(other_x, 2)
        return other_lo, other_rep, (z * 4 + other_lo * 2 + core, other_rep)

    def rep_at(step, way):
        turn, flip = step // 2, step % 2
        return 2 * lax.rem(y + (turn if way > 0 else 4 - turn), 4) + lax.rem(x_hi + flip, 2)

    def at_rep(step):
        other = rep_at(step, 1)
        return other, (grp, other)

    pair = (z * 4 + 2 * x_lo + 1 - core, rep)

    def copy(src, dst, send, recv, device):
        return pltpu.make_async_remote_copy(
            src_ref=src, dst_ref=dst, send_sem=send, recv_sem=recv,
            device_id=device, device_id_type=MESH,
        )

    def each(low, count, act):
        def turn(step, carry):
            act(step)
            return carry
        lax.fori_loop(low, count, turn, 0)

    barrier = pltpu.get_barrier_semaphore()

    def greet(device):
        pl.semaphore_signal(barrier, inc=1, device_id=device, device_id_type=MESH)

    loads = [
        pltpu.make_async_copy(src, dst, load_s.at[index])
        for index, (src, dst) in enumerate((
            (counts_h, counts), (src_degree_h, src_degree), (dst_degree_h, dst_degree),
            (inputs_h, inputs), (adjoint_h, adjoint), (active_h, active),
            (weight_h, weight),
        ))
    ]
    for load in loads[:3]:
        load.start()
    planes = {step: at_plane(step) for step in range(1, 16)}
    for step in (4, 12):
        greet(at_z(step)[1])
    for step in PLANE_FAR:
        greet(planes[step][2])
    for step in (3, 13, 2, 14, 1, 15):
        greet(at_z(step)[1])
    greet(pair)
    for load in loads[3:]:
        load.start()

    for load in loads[:3]:
        load.wait()
    src_scale = lax.rsqrt(src_degree[...].astype(F32))
    src_scale = jnp.transpose(jnp.broadcast_to(src_scale, (128, 128)))
    dst_scale = lax.rsqrt(dst_degree[...].astype(F32))
    for part in range(8):
        cols = slice(128 * part, 128 * part + 128)
        scaled = counts[:, cols].astype(F32) * src_scale * dst_scale[:, cols]
        packed[part] = scaled.astype(BF16)
    tiles[rep] = packed[rep]
    pl.semaphore_wait(barrier, 15 + 1 + 8)

    def tile_copy(step):
        other, device = at_rep(step)
        return copy(packed.at[other], tiles.at[rep], tile_s, tile_r.at[step], device)

    def tile_wait(step):
        sender = rep_at(step, -1)
        copy(packed.at[0], tiles.at[sender], tile_s, tile_r.at[step], at_rep(step)[1]).wait_recv()

    def mz_copy(step):
        piece = masked.at[z, quarter, :, columns]
        return copy(piece, piece, mz_s, mz_r, at_z(step)[1])

    def whole(ref, send, recv):
        return copy(ref, ref, send, recv, pair)

    mz_all = whole(masked.at[pl.ds(0, depth - 1), 0, :, pl.ds(0, 128)], mz_s, mz_r)
    my_all = whole(masked.at[pl.ds(0, depth), pl.ds(0, 3), :, pl.ds(0, 128)], my_s, my_r)
    mx_all = whole(masked.at[pl.ds(0, depth), 0], mx_s, mx_r)
    mc_sent = whole(masked.at[pl.ds(0, depth), pl.ds(0, 2)], mc_s, mc_r.at[0])
    tile_sent = whole(packed.at[pl.ds(0, 7)], tile_s, tile_r.at[0])
    half_sent = whole(half_out.at[pl.ds(0, 8)], half_s, half_r.at[0])
    plane_all = whole(plane_in.at[pl.ds(1, 15)], plane_s, plane_r)
    ring_all = whole(ring_in.at[pl.ds(1, depth - 1)], ring_s, ring_r)
    tot_all = whole(total.at[0, pl.ds(0, depth - 1)], tot_s, tot_r)
    cross_all = whole(total.at[0, pl.ds(0, depth)], cross_s, cross_r)
    last_sent = whole(total.at[pl.ds(0, 2)], last_s, last_r.at[0])

    def my_copy(step):
        piece = masked.at[:, quarter, :, columns]
        return copy(piece, piece, my_s, my_r, at_plane(step)[2])

    half = depth // 2

    def mx_copy(step):
        which, turn = lax.div(step, 4), lax.rem(step, 4)
        piece = masked.at[pl.ds(which * half, half), quarter, :, columns]
        return copy(piece, piece, mx_s, mx_r, at_plane(4 + 8 * which + turn)[2])

    def mc_copy(which, at):
        piece = masked.at[:, at]
        return copy(piece, piece, mc_s, mc_r.at[which], pair)

    def half_copy(step):
        return copy(half_out.at[step], half_in.at[step], half_s, half_r.at[step], pair)

    def plane_copy(step, part, owner):
        other_lo, other_rep, device = planes[step]
        rows = pl.ds(pl.multiple_of((other_lo * 8 + other_rep) * 16, 16), 16)
        return copy(plane_out.at[part, rows], plane_in.at[step, owner], plane_s, plane_r, device)

    def ring_copy(step):
        other, device = at_z(step)
        return copy(ring_out.at[other], ring_in.at[step], ring_s, ring_r, device)

    def tot_copy(step):
        piece = total.at[quarter, z]
        return copy(piece, piece, tot_s, tot_r, at_z(step)[1])

    def cross_copy(step):
        piece = total.at[quarter, z]
        return copy(piece, piece, cross_s, cross_r, at_cross(step))

    def last_copy(which, at):
        piece = total.at[at]
        return copy(piece, piece, last_s, last_r.at[which], pair)

    for step in reversed(REP_NEAR[1:]):
        tile_copy(step).start()
    for step in (4, depth - 4):
        pl.semaphore_signal(token, inc=1, device_id=at_z(step)[1], device_id_type=MESH)

    for load in loads[3:6]:
        load.wait()
    turned = jnp.transpose(inputs[...])
    for part in range(8):
        for spot in range(4):
            at = 128 * (spot // 2) + 16 * part
            inputs_t[spot % 2, at:at + 16] = turned[64 * part + 16 * spot:64 * part + 16 * spot + 16]
    columns = pl.ds(pl.multiple_of(y * 128, 128), 128)
    own = adjoint[:, columns].astype(F32) * active[:, columns].astype(F32)
    masked[z, quarter, :, columns] = own.astype(BF16)

    mine = pl.ds(pl.multiple_of((x_lo * 8 + rep) * 16, 16), 16)

    def term(side, owner):
        return lax.dot_general(
            inputs_t[side], tiles[owner], (((1,), (1,)), ((), ())), preferred_element_type=F32
        )

    def settle(step):
        owner = rep_at(REP_NEAR[step], -1)
        half_copy(step).wait_recv()
        plane_out[step] = (own_half[step] + half_in[step].astype(F32)).astype(BF16)
        for other in PLANE_FAR:
            plane_copy(other, step, owner).start()
        acc[pl.ds(pl.multiple_of(owner * 16, 16), 16)] = (
            own_half[step, mine] + half_in[step, mine].astype(F32)
        )

    for step in range(8):
        if step > 0:
            tile_wait(REP_NEAR[step])
        owner = rep_at(REP_NEAR[step], -1)
        half_out[step] = term(1 - core, owner).astype(BF16)
        half_copy(step).start()
        own_half[step] = term(core, owner)
        if step > 0:
            settle(step - 1)
        if step == 1:
            pl.semaphore_wait(token, 2)
            for other in Z_FAR:
                mz_copy(other).start()
    settle(7)

    mz_all.wait_recv()
    each(1, 4, lambda step: my_copy(step).start())
    each(0, 8, lambda step: mx_copy(step).start())

    summed = acc[...].reshape(8, 16, 128)
    plane_all.wait_recv()
    for step in range(1, 16):
        summed += plane_in[step].astype(F32)
    acc[...] = summed.reshape(128, 128)
    for row in range(depth):
        ring_out[row] = acc[pl.ds(row, 8, stride=16), :]
    for step in Z_FAR:
        ring_copy(step).start()

    my_all.wait_recv()
    mc_copy(0, quarter).start()
    mx_all.wait_recv()
    mc_copy(1, across).start()
    mc_copy(0, 2 * x_lo + 1 - core).wait_recv()
    mc_copy(1, 2 * (1 - x_lo) + 1 - core).wait_recv()

    piece = ring_out[z]
    ring_all.wait_recv()
    for step in range(1, depth):
        piece += ring_in[step]
    upper = piece.astype(BF16)
    lower = (piece - upper.astype(F32)).astype(BF16)
    both = jnp.concatenate([upper, lower], axis=0)
    which_row = lax.rem(lax.broadcasted_iota(jnp.int32, (16, 512), 0), 8)
    product = jnp.zeros((16, 512), F32)
    for part in range(8):
        block = lax.dot_general(
            both, masked[2 * part:2 * part + 2].reshape(128, 512),
            (((1,), (0,)), ((), ())), preferred_element_type=F32,
        )
        product += jnp.where(which_row == part, block, 0.0)
    total[quarter, z] = jnp.sum(product, axis=0, keepdims=True) * (1.0 / 65536.0)
    for step in Z_FAR:
        cross_copy(step).start()
        tot_copy(step).start()
    cross_copy(0).start()

    grad = jnp.zeros((128, 512), F32)
    for part in range(8):
        grad += lax.dot_general(
            jnp.transpose(tiles[part]), masked[2 * part:2 * part + 2].reshape(128, 512),
            (((1,), (0,)), ((), ())), preferred_element_type=F32,
        )
    loads[6].wait()
    grad_input[...] = lax.dot_general(
        grad.astype(BF16), weight[...], (((1,), (1,)), ((), ())), preferred_element_type=F32
    ).astype(BF16)

    for sent in (tile_sent, mz_all, my_all, mx_all, mc_sent, half_sent, plane_all, ring_all):
        sent.wait_send()

    def place(spot):
        for row in range(depth):
            sums[pl.ds(spot * depth + row, 1), :] = total[spot, row]

    tot_all.wait_recv()
    last_copy(0, quarter).start()
    cross_all.wait_recv()
    last_copy(1, across).start()
    place(quarter)
    place(across)
    tot_all.wait_send()
    cross_all.wait_send()
    last_copy(0, 2 * x_lo + 1 - core).wait_recv()
    place(2 * x_lo + 1 - core)
    last_copy(1, 2 * (1 - x_lo) + 1 - core).wait_recv()
    place(2 * (1 - x_lo) + 1 - core)
    last_sent.wait_send()


def store(near_input, near_weight, far_input, far_weight, done):
    copies = (
        pltpu.make_async_copy(near_input, far_input, done.at[0]),
        pltpu.make_async_copy(near_weight, far_weight, done.at[1]),
    )
    for copy in copies:
        copy.start()
    for copy in copies:
        copy.wait()


def body(adjoint, active, counts, src_degree, dst_degree, inputs, weight):
    dma = pltpu.SemaphoreType.DMA
    far, near = pl.BlockSpec(memory_space=pltpu.HBM), pl.BlockSpec(memory_space=pltpu.VMEM)
    sems = [dma((7,)), pltpu.SemaphoreType.REGULAR]
    for count in (8, 0, 0, 0, 2, 8, 0, 0, 0, 0, 2):
        sems += [dma, dma((count,)) if count else dma]
    I32 = jnp.int32
    results = (pltpu.VMEM((128, 512), BF16), pltpu.VMEM((64, 512), F32))
    grad_input, sums = pl.pallas_call(
        kernel,
        out_shape=results,
        in_specs=[far] * 7,
        out_specs=(near, near),
        scratch_shapes=[
            pltpu.VMEM(shape, kind) for shape, kind in (
                ((16, 512), BF16), ((16, 512), I32), ((128, 1024), I32), ((1, 128), I32),
                ((1, 1024), I32), ((128, 512), BF16), ((512, 512), BF16),
                ((16, 4, 16, 512), BF16),
                ((8, 128, 128), BF16),
                ((8, 128, 128), BF16),
                ((2, 256, 128), BF16),
                ((8, 256, 128), BF16),
                ((8, 256, 128), BF16),
                ((8, 256, 128), F32),
                ((8, 256, 128), BF16),
                ((16, 8, 16, 128), BF16),
                ((128, 128), F32),
                ((16, 8, 128), F32),
                ((16, 8, 128), F32),
                ((4, 16, 1, 512), F32),
            )
        ] + sems,
        compiler_params=pltpu.CompilerParams(
            collective_id=0, has_side_effects=True, vmem_limit_bytes=56 * 1024 * 1024
        ),
    )(
        adjoint, active, counts, src_degree.reshape(1, 128), dst_degree.reshape(1, 1024), inputs,
        weight,
    )
    return tuple(pl.pallas_call(
        store,
        out_shape=(
            jax.ShapeDtypeStruct((128, 512), BF16),
            jax.ShapeDtypeStruct((64, 512), F32),
        ),
        in_specs=[near, near],
        out_specs=(far, far),
        scratch_shapes=[dma((2,))], compiler_params=pltpu.CompilerParams(vmem_limit_bytes=1024 * 1024),
    )(grad_input, sums))


def solution(mesh):
    in_specs = (
        P("grp", None),
        P("grp", None),
        P("rep", "grp"),
        P("rep"),
        P("grp"),
        P(("grp", "rep"), None),
        P(),
    )
    out_specs = (P(("grp", "rep"), None), P("rep", None))
    return jax.shard_map(body, mesh=mesh, in_specs=in_specs, out_specs=out_specs, check_vma=False)
```

```python
import jax
import jax.numpy as jnp
from jax import lax
from jax.experimental import pallas as pl
from jax.experimental.pallas import tpu as pltpu
from jax.sharding import PartitionSpec as P

MESH = pl.DeviceIdType.MESH
F32, BF16 = jnp.float32, jnp.bfloat16


def ring_far(step, size):
    return min(step, size - step)


PLANE_FAR = sorted(range(1, 16), key=lambda step: -ring_far(step // 4, 4) - ring_far(step % 4, 4))
Z_FAR = sorted(range(1, 16), key=lambda step: -ring_far(step, 16))
REP_NEAR = sorted(range(8), key=lambda step: ring_far(step // 2, 4) + 2 * (step % 2))


def kernel(
    adjoint_h, active_h, counts_h, src_degree_h, dst_degree_h, inputs_h, weight_h,
    grad_input, sums,
    adjoint, active, counts, src_degree, dst_degree, inputs, weight,
    masked, packed, tiles, inputs_t, half_out, half_in, own_half, plane_out, plane_in,
    acc, ring_out, ring_in, total,
    load_s, token,
    tile_s, tile_r, mz_s, mz_r, my_s, my_r, mx_s, mx_r, mc_s, mc_r,
    half_s, half_r, plane_s, plane_r, ring_s, ring_r, tot_s, tot_r, cross_s, cross_r, last_s, last_r,
):
    grp, rep = lax.axis_index("grp"), lax.axis_index("rep")
    depth = masked.shape[0]
    z, quarter = lax.div(grp, 4), lax.rem(grp, 4)
    x_lo, core = lax.div(quarter, 2), lax.rem(quarter, 2)
    y, x_hi = lax.div(rep, 2), lax.rem(rep, 2)
    x = 2 * x_hi + x_lo
    across = 2 * (1 - x_lo) + core

    def at_z(step):
        other = lax.rem(z + step, depth)
        return other, (other * 4 + quarter, rep)

    def at_cross(step):
        return (lax.rem(z + step, depth) * 4 + across, rep)

    def at_plane(step):
        other_x, other_y = lax.rem(x + lax.div(step, 4), 4), lax.rem(y + lax.rem(step, 4), 4)
        other_lo = lax.rem(other_x, 2)
        other_rep = 2 * other_y + lax.div(other_x, 2)
        return other_lo, other_rep, (z * 4 + other_lo * 2 + core, other_rep)

    def rep_at(step, way):
        turn, flip = step // 2, step % 2
        return 2 * lax.rem(y + (turn if way > 0 else 4 - turn), 4) + lax.rem(x_hi + flip, 2)

    def at_rep(step):
        other = rep_at(step, 1)
        return other, (grp, other)

    pair = (z * 4 + 2 * x_lo + 1 - core, rep)

    def copy(src, dst, send, recv, device):
        return pltpu.make_async_remote_copy(
            src_ref=src, dst_ref=dst, send_sem=send, recv_sem=recv,
            device_id=device, device_id_type=MESH,
        )

    def each(low, count, act):
        def turn(step, carry):
            act(step)
            return carry
        lax.fori_loop(low, count, turn, 0)

    barrier = pltpu.get_barrier_semaphore()

    def greet(device):
        pl.semaphore_signal(barrier, inc=1, device_id=device, device_id_type=MESH)

    loads = [
        pltpu.make_async_copy(src, dst, load_s.at[index])
        for index, (src, dst) in enumerate((
            (counts_h, counts), (src_degree_h, src_degree), (dst_degree_h, dst_degree),
            (inputs_h, inputs), (adjoint_h, adjoint), (active_h, active),
            (weight_h, weight),
        ))
    ]
    for load in loads[:3]:
        load.start()
    planes = {step: at_plane(step) for step in range(1, 16)}
    for step in (4, 12):
        greet(at_z(step)[1])
    for step in PLANE_FAR:
        greet(planes[step][2])
    for step in (3, 13, 2, 14, 1, 15):
        greet(at_z(step)[1])
    greet(pair)
    for load in loads[3:]:
        load.start()

    for load in loads[:3]:
        load.wait()
    src_scale = lax.rsqrt(src_degree[...].astype(F32))
    src_scale = jnp.transpose(jnp.broadcast_to(src_scale, (128, 128)))
    dst_scale = lax.rsqrt(dst_degree[...].astype(F32))
    for part in range(8):
        cols = slice(128 * part, 128 * part + 128)
        scaled = counts[:, cols].astype(F32) * src_scale * dst_scale[:, cols]
        packed[part] = scaled.astype(BF16)
    tiles[rep] = packed[rep]
    pl.semaphore_wait(barrier, 15 + 1 + 8)

    def tile_copy(step):
        other, device = at_rep(step)
        return copy(packed.at[other], tiles.at[rep], tile_s, tile_r.at[step], device)

    def tile_wait(step):
        sender = rep_at(step, -1)
        copy(packed.at[0], tiles.at[sender], tile_s, tile_r.at[step], at_rep(step)[1]).wait_recv()

    def mz_copy(step):
        piece = masked.at[z, quarter, :, columns]
        return copy(piece, piece, mz_s, mz_r, at_z(step)[1])

    def whole(ref, send, recv):
        return copy(ref, ref, send, recv, pair)

    mz_all = whole(masked.at[pl.ds(0, depth - 1), 0, :, pl.ds(0, 128)], mz_s, mz_r)
    my_all = whole(masked.at[pl.ds(0, depth), pl.ds(0, 3), :, pl.ds(0, 128)], my_s, my_r)
    mx_all = whole(masked.at[pl.ds(0, depth), 0], mx_s, mx_r)
    mc_sent = whole(masked.at[pl.ds(0, depth), pl.ds(0, 2)], mc_s, mc_r.at[0])
    tile_sent = whole(packed.at[pl.ds(0, 7)], tile_s, tile_r.at[0])
    half_sent = whole(half_out.at[pl.ds(0, 8)], half_s, half_r.at[0])
    plane_all = whole(plane_in.at[pl.ds(1, 15)], plane_s, plane_r)
    ring_all = whole(ring_in.at[pl.ds(1, depth - 1)], ring_s, ring_r)
    tot_all = whole(total.at[0, pl.ds(0, depth - 1)], tot_s, tot_r)
    cross_all = whole(total.at[0, pl.ds(0, depth)], cross_s, cross_r)
    last_sent = whole(total.at[pl.ds(0, 2)], last_s, last_r.at[0])

    def my_copy(step):
        piece = masked.at[:, quarter, :, columns]
        return copy(piece, piece, my_s, my_r, at_plane(step)[2])

    half = depth // 2

    def mx_copy(step):
        which, turn = lax.div(step, 4), lax.rem(step, 4)
        piece = masked.at[pl.ds(which * half, half), quarter, :, columns]
        return copy(piece, piece, mx_s, mx_r, at_plane(4 + 8 * which + turn)[2])

    def mc_copy(which, at):
        piece = masked.at[:, at]
        return copy(piece, piece, mc_s, mc_r.at[which], pair)

    def half_copy(step):
        return copy(half_out.at[step], half_in.at[step], half_s, half_r.at[step], pair)

    def plane_copy(step, part, owner):
        other_lo, other_rep, device = planes[step]
        rows = pl.ds(pl.multiple_of((other_lo * 8 + other_rep) * 16, 16), 16)
        return copy(plane_out.at[part, rows], plane_in.at[step, owner], plane_s, plane_r, device)

    def ring_copy(step):
        other, device = at_z(step)
        return copy(ring_out.at[other], ring_in.at[step], ring_s, ring_r, device)

    def tot_copy(step):
        piece = total.at[quarter, z]
        return copy(piece, piece, tot_s, tot_r, at_z(step)[1])

    def cross_copy(step):
        piece = total.at[quarter, z]
        return copy(piece, piece, cross_s, cross_r, at_cross(step))

    def last_copy(which, at):
        piece = total.at[at]
        return copy(piece, piece, last_s, last_r.at[which], pair)

    for step in reversed(REP_NEAR[1:]):
        tile_copy(step).start()
    for step in (4, depth - 4):
        pl.semaphore_signal(token, inc=1, device_id=at_z(step)[1], device_id_type=MESH)

    for load in loads[3:6]:
        load.wait()
    turned = jnp.transpose(inputs[...])
    for part in range(8):
        for spot in range(4):
            at = 128 * (spot // 2) + 16 * part
            inputs_t[spot % 2, at:at + 16] = turned[64 * part + 16 * spot:64 * part + 16 * spot + 16]
    columns = pl.ds(pl.multiple_of(y * 128, 128), 128)
    own = adjoint[:, columns].astype(F32) * active[:, columns].astype(F32)
    masked[z, quarter, :, columns] = own.astype(BF16)
    for step in Z_FAR[7:]:
        mz_copy(step).start()

    mine = pl.ds(pl.multiple_of((x_lo * 8 + rep) * 16, 16), 16)

    def term(side, owner):
        return lax.dot_general(
            inputs_t[side], tiles[owner], (((1,), (1,)), ((), ())), preferred_element_type=F32
        )

    def settle(step):
        owner = rep_at(REP_NEAR[step], -1)
        half_copy(step).wait_recv()
        plane_out[step] = (own_half[step] + half_in[step].astype(F32)).astype(BF16)
        for other in PLANE_FAR:
            plane_copy(other, step, owner).start()
        acc[pl.ds(pl.multiple_of(owner * 16, 16), 16)] = (
            own_half[step, mine] + half_in[step, mine].astype(F32)
        )

    for step in range(8):
        if step > 0:
            tile_wait(REP_NEAR[step])
        owner = rep_at(REP_NEAR[step], -1)
        half_out[step] = term(1 - core, owner).astype(BF16)
        half_copy(step).start()
        own_half[step] = term(core, owner)
        if step > 0:
            settle(step - 1)
        if step == 1:
            pl.semaphore_wait(token, 2)
            for other in Z_FAR[:7]:
                mz_copy(other).start()
    settle(7)

    mz_all.wait_recv()
    each(1, 4, lambda step: my_copy(step).start())
    each(0, 8, lambda step: mx_copy(step).start())

    summed = acc[...].reshape(8, 16, 128)
    plane_all.wait_recv()
    for step in range(1, 16):
        summed += plane_in[step].astype(F32)
    acc[...] = summed.reshape(128, 128)
    for row in range(depth):
        ring_out[row] = acc[pl.ds(row, 8, stride=16), :].astype(BF16)
    for step in Z_FAR:
        ring_copy(step).start()

    my_all.wait_recv()
    mc_copy(0, quarter).start()
    mx_all.wait_recv()
    mc_copy(1, across).start()
    mc_copy(0, 2 * x_lo + 1 - core).wait_recv()
    mc_copy(1, 2 * (1 - x_lo) + 1 - core).wait_recv()

    piece = acc[pl.ds(z, 8, stride=16), :]
    ring_all.wait_recv()
    for step in range(1, depth):
        piece += ring_in[step].astype(F32)
    upper = piece.astype(BF16)
    lower = (piece - upper.astype(F32)).astype(BF16)
    both = jnp.concatenate([upper, lower], axis=0)
    which_row = lax.rem(lax.broadcasted_iota(jnp.int32, (16, 512), 0), 8)
    product = jnp.zeros((16, 512), F32)
    for part in range(8):
        block = lax.dot_general(
            both, masked[2 * part:2 * part + 2].reshape(128, 512),
            (((1,), (0,)), ((), ())), preferred_element_type=F32,
        )
        product += jnp.where(which_row == part, block, 0.0)
    total[quarter, z] = jnp.sum(product, axis=0, keepdims=True) * (1.0 / 65536.0)
    for step in Z_FAR:
        cross_copy(step).start()
        tot_copy(step).start()
    cross_copy(0).start()

    grad = jnp.zeros((128, 512), F32)
    for part in range(8):
        grad += lax.dot_general(
            jnp.transpose(tiles[part]), masked[2 * part:2 * part + 2].reshape(128, 512),
            (((1,), (0,)), ((), ())), preferred_element_type=F32,
        )
    loads[6].wait()
    grad_input[...] = lax.dot_general(
        grad.astype(BF16), weight[...], (((1,), (1,)), ((), ())), preferred_element_type=F32
    ).astype(BF16)

    for sent in (tile_sent, mz_all, my_all, mx_all, mc_sent, half_sent, plane_all, ring_all):
        sent.wait_send()

    def place(spot):
        for row in range(depth):
            sums[pl.ds(spot * depth + row, 1), :] = total[spot, row]

    tot_all.wait_recv()
    last_copy(0, quarter).start()
    cross_all.wait_recv()
    last_copy(1, across).start()
    place(quarter)
    place(across)
    tot_all.wait_send()
    cross_all.wait_send()
    last_copy(0, 2 * x_lo + 1 - core).wait_recv()
    place(2 * x_lo + 1 - core)
    last_copy(1, 2 * (1 - x_lo) + 1 - core).wait_recv()
    place(2 * (1 - x_lo) + 1 - core)
    last_sent.wait_send()


def store(near_input, near_weight, far_input, far_weight, done):
    copies = (
        pltpu.make_async_copy(near_input, far_input, done.at[0]),
        pltpu.make_async_copy(near_weight, far_weight, done.at[1]),
    )
    for copy in copies:
        copy.start()
    for copy in copies:
        copy.wait()


def body(adjoint, active, counts, src_degree, dst_degree, inputs, weight):
    dma = pltpu.SemaphoreType.DMA
    far, near = pl.BlockSpec(memory_space=pltpu.HBM), pl.BlockSpec(memory_space=pltpu.VMEM)
    sems = [dma((7,)), pltpu.SemaphoreType.REGULAR]
    for count in (8, 0, 0, 0, 2, 8, 0, 0, 0, 0, 2):
        sems += [dma, dma((count,)) if count else dma]
    I32 = jnp.int32
    results = (pltpu.VMEM((128, 512), BF16), pltpu.VMEM((64, 512), F32))
    grad_input, sums = pl.pallas_call(
        kernel,
        out_shape=results,
        in_specs=[far] * 7,
        out_specs=(near, near),
        scratch_shapes=[
            pltpu.VMEM(shape, kind) for shape, kind in (
                ((16, 512), BF16), ((16, 512), I32), ((128, 1024), I32), ((1, 128), I32),
                ((1, 1024), I32), ((128, 512), BF16), ((512, 512), BF16),
                ((16, 4, 16, 512), BF16),
                ((8, 128, 128), BF16),
                ((8, 128, 128), BF16),
                ((2, 256, 128), BF16),
                ((8, 256, 128), BF16),
                ((8, 256, 128), BF16),
                ((8, 256, 128), F32),
                ((8, 256, 128), BF16),
                ((16, 8, 16, 128), BF16),
                ((128, 128), F32),
                ((16, 8, 128), BF16),
                ((16, 8, 128), BF16),
                ((4, 16, 1, 512), F32),
            )
        ] + sems,
        compiler_params=pltpu.CompilerParams(
            collective_id=0, has_side_effects=True, vmem_limit_bytes=56 * 1024 * 1024
        ),
    )(
        adjoint, active, counts, src_degree.reshape(1, 128), dst_degree.reshape(1, 1024), inputs,
        weight,
    )
    return tuple(pl.pallas_call(
        store,
        out_shape=(
            jax.ShapeDtypeStruct((128, 512), BF16),
            jax.ShapeDtypeStruct((64, 512), F32),
        ),
        in_specs=[near, near],
        out_specs=(far, far),
        scratch_shapes=[dma((2,))], compiler_params=pltpu.CompilerParams(vmem_limit_bytes=1024 * 1024),
    )(grad_input, sums))


def solution(mesh):
    in_specs = (
        P("grp", None),
        P("grp", None),
        P("rep", "grp"),
        P("rep"),
        P("grp"),
        P(("grp", "rep"), None),
        P(),
    )
    out_specs = (P(("grp", "rep"), None), P("rep", None))
    return jax.shard_map(body, mesh=mesh, in_specs=in_specs, out_specs=out_specs, check_vma=False)
```

```python
import jax
import jax.numpy as jnp
from jax import lax
from jax.experimental import pallas as pl
from jax.experimental.pallas import tpu as pltpu
from jax.sharding import PartitionSpec as P

MESH = pl.DeviceIdType.MESH
F32, BF16 = jnp.float32, jnp.bfloat16


def ring_far(step, size):
    return min(step, size - step)


PLANE_FAR = sorted(range(1, 16), key=lambda step: -ring_far(step // 4, 4) - ring_far(step % 4, 4))
Z_FAR = sorted(range(1, 16), key=lambda step: -ring_far(step, 16))
REP_NEAR = sorted(range(8), key=lambda step: ring_far(step // 2, 4) + 2 * (step % 2))


def kernel(
    adjoint_h, active_h, counts_h, src_degree_h, dst_degree_h, inputs_h, weight_h,
    grad_input, sums,
    adjoint, active, counts, src_degree, dst_degree, inputs, weight,
    masked, packed, tiles, inputs_t, half_out, half_in, own_half, plane_out, plane_in,
    acc, ring_out, ring_in, total,
    load_s, token,
    tile_s, tile_r, mz_s, mz_r, my_s, my_r, mx_s, mx_r, mc_s, mc_r,
    half_s, half_r, plane_s, plane_r, ring_s, ring_r, tot_s, tot_r, cross_s, cross_r, last_s, last_r,
):
    grp, rep = lax.axis_index("grp"), lax.axis_index("rep")
    depth = masked.shape[0]
    z, quarter = lax.div(grp, 4), lax.rem(grp, 4)
    x_lo, core = lax.div(quarter, 2), lax.rem(quarter, 2)
    y, x_hi = lax.div(rep, 2), lax.rem(rep, 2)
    x = 2 * x_hi + x_lo
    across = 2 * (1 - x_lo) + core

    def at_z(step):
        other = lax.rem(z + step, depth)
        return other, (other * 4 + quarter, rep)

    def at_cross(step):
        return (lax.rem(z + step, depth) * 4 + across, rep)

    def at_plane(step):
        other_x, other_y = lax.rem(x + lax.div(step, 4), 4), lax.rem(y + lax.rem(step, 4), 4)
        other_lo = lax.rem(other_x, 2)
        other_rep = 2 * other_y + lax.div(other_x, 2)
        return other_lo, other_rep, (z * 4 + other_lo * 2 + core, other_rep)

    def rep_at(step, way):
        turn, flip = step // 2, step % 2
        return 2 * lax.rem(y + (turn if way > 0 else 4 - turn), 4) + lax.rem(x_hi + flip, 2)

    def at_rep(step):
        other = rep_at(step, 1)
        return other, (grp, other)

    pair = (z * 4 + 2 * x_lo + 1 - core, rep)

    def copy(src, dst, send, recv, device):
        return pltpu.make_async_remote_copy(
            src_ref=src, dst_ref=dst, send_sem=send, recv_sem=recv,
            device_id=device, device_id_type=MESH,
        )

    def each(low, count, act):
        def turn(step, carry):
            act(step)
            return carry
        lax.fori_loop(low, count, turn, 0)

    barrier = pltpu.get_barrier_semaphore()

    def greet(device):
        pl.semaphore_signal(barrier, inc=1, device_id=device, device_id_type=MESH)

    loads = [
        pltpu.make_async_copy(src, dst, load_s.at[index])
        for index, (src, dst) in enumerate((
            (counts_h, counts), (src_degree_h, src_degree), (dst_degree_h, dst_degree),
            (inputs_h, inputs), (adjoint_h, adjoint), (active_h, active),
            (weight_h, weight),
        ))
    ]
    for load in loads[:3]:
        load.start()
    planes = {step: at_plane(step) for step in range(1, 16)}
    for step in (4, 12):
        greet(at_z(step)[1])
    for step in PLANE_FAR:
        greet(planes[step][2])
    for step in (3, 13, 2, 14, 1, 15):
        greet(at_z(step)[1])
    greet(pair)
    for load in loads[3:]:
        load.start()

    for load in loads[:3]:
        load.wait()
    src_scale = lax.rsqrt(src_degree[...].astype(F32))
    src_scale = jnp.transpose(jnp.broadcast_to(src_scale, (128, 128)))
    dst_scale = lax.rsqrt(dst_degree[...].astype(F32))
    for part in range(8):
        cols = slice(128 * part, 128 * part + 128)
        scaled = counts[:, cols].astype(F32) * src_scale * dst_scale[:, cols]
        packed[part] = scaled.astype(BF16)
    tiles[rep] = packed[rep]
    pl.semaphore_wait(barrier, 15 + 1 + 8)

    def tile_copy(step):
        other, device = at_rep(step)
        return copy(packed.at[other], tiles.at[rep], tile_s, tile_r.at[step], device)

    def tile_wait(step):
        sender = rep_at(step, -1)
        copy(packed.at[0], tiles.at[sender], tile_s, tile_r.at[step], at_rep(step)[1]).wait_recv()

    def mz_copy(step):
        piece = masked.at[z, quarter, :, columns]
        return copy(piece, piece, mz_s, mz_r, at_z(step)[1])

    def whole(ref, send, recv):
        return copy(ref, ref, send, recv, pair)

    mz_all = whole(masked.at[pl.ds(0, depth - 1), 0, :, pl.ds(0, 128)], mz_s, mz_r)
    my_all = whole(masked.at[pl.ds(0, depth), pl.ds(0, 3), :, pl.ds(0, 128)], my_s, my_r)
    mx_all = whole(masked.at[pl.ds(0, depth), 0], mx_s, mx_r)
    mc_sent = whole(masked.at[pl.ds(0, depth), pl.ds(0, 2)], mc_s, mc_r.at[0])
    tile_sent = whole(packed.at[pl.ds(0, 7)], tile_s, tile_r.at[0])
    half_sent = whole(half_out.at[pl.ds(0, 8)], half_s, half_r.at[0])
    plane_all = whole(plane_in.at[pl.ds(1, 15)], plane_s, plane_r)
    ring_all = whole(ring_in.at[pl.ds(1, depth - 1)], ring_s, ring_r)
    tot_all = whole(total.at[0, pl.ds(0, depth - 1)], tot_s, tot_r)
    cross_all = whole(total.at[0, pl.ds(0, depth)], cross_s, cross_r)
    last_sent = whole(total.at[pl.ds(0, 2)], last_s, last_r.at[0])

    def my_copy(step):
        piece = masked.at[:, quarter, :, columns]
        return copy(piece, piece, my_s, my_r, at_plane(step)[2])

    half = depth // 2

    def mx_copy(step):
        which, turn = lax.div(step, 4), lax.rem(step, 4)
        piece = masked.at[pl.ds(which * half, half), quarter, :, columns]
        return copy(piece, piece, mx_s, mx_r, at_plane(4 + 8 * which + turn)[2])

    def mc_copy(which, at):
        piece = masked.at[:, at]
        return copy(piece, piece, mc_s, mc_r.at[which], pair)

    def half_copy(step):
        return copy(half_out.at[step], half_in.at[step], half_s, half_r.at[step], pair)

    def plane_copy(step, part, owner):
        other_lo, other_rep, device = planes[step]
        rows = pl.ds(pl.multiple_of((other_lo * 8 + other_rep) * 16, 16), 16)
        return copy(plane_out.at[part, rows], plane_in.at[step, owner], plane_s, plane_r, device)

    def ring_copy(step):
        other, device = at_z(step)
        return copy(ring_out.at[other], ring_in.at[step], ring_s, ring_r, device)

    def tot_copy(step):
        piece = total.at[quarter, z]
        return copy(piece, piece, tot_s, tot_r, at_z(step)[1])

    def cross_copy(step):
        piece = total.at[quarter, z]
        return copy(piece, piece, cross_s, cross_r, at_cross(step))

    def last_copy(which, at):
        piece = total.at[at]
        return copy(piece, piece, last_s, last_r.at[which], pair)

    for step in reversed(REP_NEAR[1:]):
        tile_copy(step).start()
    for step in (4, depth - 4):
        pl.semaphore_signal(token, inc=1, device_id=at_z(step)[1], device_id_type=MESH)

    for load in loads[3:6]:
        load.wait()
    turned = jnp.transpose(inputs[...])
    for part in range(8):
        for spot in range(4):
            at = 128 * (spot // 2) + 16 * part
            inputs_t[spot % 2, at:at + 16] = turned[64 * part + 16 * spot:64 * part + 16 * spot + 16]
    columns = pl.ds(pl.multiple_of(y * 128, 128), 128)
    own = adjoint[:, columns].astype(F32) * active[:, columns].astype(F32)
    masked[z, quarter, :, columns] = own.astype(BF16)
    for step in Z_FAR[7:]:
        mz_copy(step).start()

    mine = pl.ds(pl.multiple_of((x_lo * 8 + rep) * 16, 16), 16)

    def term(side, owner):
        return lax.dot_general(
            inputs_t[side], tiles[owner], (((1,), (1,)), ((), ())), preferred_element_type=F32
        )

    def settle(step):
        owner = rep_at(REP_NEAR[step], -1)
        half_copy(step).wait_recv()
        plane_out[step] = (own_half[step] + half_in[step].astype(F32)).astype(BF16)
        for other in PLANE_FAR:
            plane_copy(other, step, owner).start()
        acc[pl.ds(pl.multiple_of(owner * 16, 16), 16)] = (
            own_half[step, mine] + half_in[step, mine].astype(F32)
        )

    for step in range(8):
        if step > 0:
            tile_wait(REP_NEAR[step])
        owner = rep_at(REP_NEAR[step], -1)
        half_out[step] = term(1 - core, owner).astype(BF16)
        half_copy(step).start()
        own_half[step] = term(core, owner)
        if step > 0:
            settle(step - 1)
        if step == 1:
            pl.semaphore_wait(token, 2)
            for other in Z_FAR[:7]:
                mz_copy(other).start()
    settle(7)

    mz_all.wait_recv()
    each(1, 4, lambda step: my_copy(step).start())
    each(0, 8, lambda step: mx_copy(step).start())

    summed = acc[...].reshape(8, 16, 128)
    plane_all.wait_recv()
    for step in range(1, 16):
        summed += plane_in[step].astype(F32)
    acc[...] = summed.reshape(128, 128)
    for row in range(depth):
        ring_out[row] = acc[pl.ds(row, 8, stride=16), :]
    for step in Z_FAR:
        ring_copy(step).start()

    my_all.wait_recv()
    mc_copy(0, quarter).start()
    mx_all.wait_recv()
    mc_copy(1, across).start()
    mc_copy(0, 2 * x_lo + 1 - core).wait_recv()
    mc_copy(1, 2 * (1 - x_lo) + 1 - core).wait_recv()

    piece = ring_out[z]
    ring_all.wait_recv()
    for step in range(1, depth):
        piece += ring_in[step]
    upper = piece.astype(BF16)
    lower = (piece - upper.astype(F32)).astype(BF16)
    both = jnp.concatenate([upper, lower], axis=0)
    which_row = lax.rem(lax.broadcasted_iota(jnp.int32, (16, 512), 0), 8)
    product = jnp.zeros((16, 512), F32)
    for part in range(8):
        block = lax.dot_general(
            both, masked[2 * part:2 * part + 2].reshape(128, 512),
            (((1,), (0,)), ((), ())), preferred_element_type=F32,
        )
        product += jnp.where(which_row == part, block, 0.0)
    total[quarter, z] = jnp.sum(product, axis=0, keepdims=True) * (1.0 / 65536.0)
    for step in Z_FAR:
        cross_copy(step).start()
        tot_copy(step).start()
    cross_copy(0).start()

    grad = jnp.zeros((128, 512), F32)
    for part in range(8):
        grad += lax.dot_general(
            jnp.transpose(tiles[part]), masked[2 * part:2 * part + 2].reshape(128, 512),
            (((1,), (0,)), ((), ())), preferred_element_type=F32,
        )
    loads[6].wait()
    grad_input[...] = lax.dot_general(
        grad.astype(BF16), weight[...], (((1,), (1,)), ((), ())), preferred_element_type=F32
    ).astype(BF16)

    for sent in (tile_sent, mz_all, my_all, mx_all, mc_sent, half_sent, plane_all, ring_all):
        sent.wait_send()

    def place(spot):
        for row in range(depth):
            sums[pl.ds(spot * depth + row, 1), :] = total[spot, row]

    tot_all.wait_recv()
    last_copy(0, quarter).start()
    cross_all.wait_recv()
    last_copy(1, across).start()
    place(quarter)
    place(across)
    tot_all.wait_send()
    cross_all.wait_send()
    last_copy(0, 2 * x_lo + 1 - core).wait_recv()
    place(2 * x_lo + 1 - core)
    last_copy(1, 2 * (1 - x_lo) + 1 - core).wait_recv()
    place(2 * (1 - x_lo) + 1 - core)
    last_sent.wait_send()


def store(near_input, near_weight, far_input, far_weight, done):
    copies = (
        pltpu.make_async_copy(near_input, far_input, done.at[0]),
        pltpu.make_async_copy(near_weight, far_weight, done.at[1]),
    )
    for copy in copies:
        copy.start()
    for copy in copies:
        copy.wait()


def body(adjoint, active, counts, src_degree, dst_degree, inputs, weight):
    dma = pltpu.SemaphoreType.DMA
    far, near = pl.BlockSpec(memory_space=pltpu.HBM), pl.BlockSpec(memory_space=pltpu.VMEM)
    sems = [dma((7,)), pltpu.SemaphoreType.REGULAR]
    for count in (8, 0, 0, 0, 2, 8, 0, 0, 0, 0, 2):
        sems += [dma, dma((count,)) if count else dma]
    I32 = jnp.int32
    results = (pltpu.VMEM((128, 512), BF16), pltpu.VMEM((64, 512), F32))
    grad_input, sums = pl.pallas_call(
        kernel,
        out_shape=results,
        in_specs=[far] * 7,
        out_specs=(near, near),
        scratch_shapes=[
            pltpu.VMEM(shape, kind) for shape, kind in (
                ((16, 512), BF16), ((16, 512), I32), ((128, 1024), I32), ((1, 128), I32),
                ((1, 1024), I32), ((128, 512), BF16), ((512, 512), BF16),
                ((16, 4, 16, 512), BF16),
                ((8, 128, 128), BF16),
                ((8, 128, 128), BF16),
                ((2, 256, 128), BF16),
                ((8, 256, 128), BF16),
                ((8, 256, 128), BF16),
                ((8, 256, 128), F32),
                ((8, 256, 128), BF16),
                ((16, 8, 16, 128), BF16),
                ((128, 128), F32),
                ((16, 8, 128), F32),
                ((16, 8, 128), F32),
                ((4, 16, 1, 512), F32),
            )
        ] + sems,
        compiler_params=pltpu.CompilerParams(
            collective_id=0, has_side_effects=True, vmem_limit_bytes=56 * 1024 * 1024
        ),
    )(
        adjoint, active, counts, src_degree.reshape(1, 128), dst_degree.reshape(1, 1024), inputs,
        weight,
    )
    return tuple(pl.pallas_call(
        store,
        out_shape=(
            jax.ShapeDtypeStruct((128, 512), BF16),
            jax.ShapeDtypeStruct((64, 512), F32),
        ),
        in_specs=[near, near],
        out_specs=(far, far),
        scratch_shapes=[dma((2,))], compiler_params=pltpu.CompilerParams(vmem_limit_bytes=1024 * 1024),
    )(grad_input, sums))


def solution(mesh):
    in_specs = (
        P("grp", None),
        P("grp", None),
        P("rep", "grp"),
        P("rep"),
        P("grp"),
        P(("grp", "rep"), None),
        P(),
    )
    out_specs = (P(("grp", "rep"), None), P("rep", None))
    return jax.shard_map(body, mesh=mesh, in_specs=in_specs, out_specs=out_specs, check_vma=False)
```
